32 devices in a mesh: grp: 1, head: 16 (over z, x, core), tile: 2 (over y).
Axes of the slice: x: 2, y: 2, z: 4, core: 2. Of those that a mesh axis runs over, the one named last changes fastest.
Arguments:
- attention: bfloat16 [144, 256, 256], P(('grp', 'head'), None, 'tile'), may hold values from 0 to 16, as said below
- proj_weight: bfloat16 [64, 144], replicated, may hold values from -0.5 to 0.5
- proj_bias: float32 [64], replicated, may hold values from -1.8 to 1.8
- conv_weight: bfloat16 [2, 2, 64, 64, 3, 3], replicated, may hold values from -0.25 to 0.25
- conv_bias: float32 [2, 2, 64], replicated, may hold values from -1.8 to 1.8
- out_weight: float32 [64], replicated, may hold values from -0.75 to 0.75
Outputs:
- logits: float32 [256, 256], P(('grp', 'head'), 'tile')
The draws below stay inside these ranges and needn't reach their ends.
Inputs may be any that keep to these rules, and one draw needn't show every extreme that they name: `attention`: every entry is positive.
All inputs are finite; a program needn't handle non-finite values.
Results may differ from the reference program's by a relative error of at most 0.007.
Values may be sent and summed in bfloat16 or wider, within the bound.
A program may use at most 128 MiB of HBM per device.

```python
import math
import jax
import jax.numpy as jnp
from jax import lax

MAPS = 144
FEAT = 64
BLOCKS = 2
W = 256


def draw_attention(key, part):
    keys = jax.random.split(jax.random.fold_in(key, 17), 4)
    row_scale = jnp.exp(jax.random.uniform(keys[0], (MAPS, W, 1), jnp.float32, 0.0, math.log(10.0)))
    col_scale = jnp.exp(jax.random.uniform(keys[1], (MAPS, 1, W), jnp.float32, 0.0, math.log(10.0)))
    entries = jax.random.uniform(keys[3], (MAPS, W, W), jnp.float32, 0.05, 1.0)
    return (row_scale * col_scale * entries / 16.0).astype(jnp.bfloat16)


def gaussian(key, extent, scale, most, dtype=jnp.bfloat16):
    return jnp.clip(scale * jax.random.normal(key, extent, jnp.float32), -most, most).astype(dtype)


def setup_inputs(seed: int = 0, part: int = 0) -> dict:
    streams_of = jax.random.split(jax.random.key(seed), 7)
    part_splits = jax.random.split(jax.random.fold_in(streams_of[6], part), 7)
    attention = draw_attention(jax.random.fold_in(jax.random.fold_in(streams_of[6], part), 71), part)
    proj_weight = gaussian(streams_of[1], (FEAT, MAPS), MAPS ** -0.5, 0.5)
    proj_bias = gaussian(streams_of[2], (FEAT,), 0.3, 1.8, jnp.float32)
    conv_weight = gaussian(streams_of[3], (BLOCKS, 2, FEAT, FEAT, 3, 3), (9 * FEAT) ** -0.5, 0.25)
    conv_bias = gaussian(streams_of[4], (BLOCKS, 2, FEAT), 0.3, 1.8, jnp.float32)
    out_weight = gaussian(streams_of[5], (FEAT,), FEAT ** -0.5, 0.75, jnp.float32)
    return dict(attention=attention, proj_weight=proj_weight, proj_bias=proj_bias, conv_weight=conv_weight, conv_bias=conv_bias, out_weight=out_weight)


def convolve(field, kernel, offsets):
    result = lax.conv_general_dilated(field[None], kernel.astype(jnp.float32), (1, 1), ((1, 1), (1, 1)), precision=lax.Precision.HIGHEST)[0]
    return result + offsets[:, None, None]


def reference(attention, proj_weight, proj_bias, conv_weight, conv_bias, out_weight):
    values = attention.astype(jnp.float32)
    symmetric = values + jnp.swapaxes(values, 1, 2)
    rowsum = jnp.sum(symmetric, axis=2)
    grand_total = jnp.sum(rowsum, axis=1)
    corrected = (symmetric - rowsum[:, :, None] * rowsum[:, None, :] / grand_total[:, None, None]).astype(jnp.bfloat16)
    stream = jnp.einsum('kc,crs->krs', proj_weight.astype(jnp.float32), corrected.astype(jnp.float32), precision=lax.Precision.HIGHEST)
    stream = (stream + proj_bias[:, None, None]).astype(jnp.bfloat16)
    for layer_index in range(BLOCKS):
        hidden = jax.nn.elu(convolve(stream.astype(jnp.float32), conv_weight[layer_index, 0], conv_bias[layer_index, 0])).astype(jnp.bfloat16)
        update = convolve(hidden.astype(jnp.float32), conv_weight[layer_index, 1], conv_bias[layer_index, 1])
        stream = (stream.astype(jnp.float32) + update).astype(jnp.bfloat16)
    return jnp.einsum('k,krs->rs', out_weight, stream.astype(jnp.float32), precision=lax.Precision.HIGHEST)
```

```python
import functools
import jax
import jax.numpy as jnp
from jax import lax
from jax.experimental import pallas as pl
from jax.experimental.pallas import tpu as pltpu
from jax.sharding import PartitionSpec as P

VM = pltpu.VMEM


def remote(src, dst, send, recv, head, tile):
    return pltpu.make_async_remote_copy(
        src_ref=src,
        dst_ref=dst,
        send_sem=send,
        recv_sem=recv,
        device_id={"head": head, "tile": tile},
        device_id_type=pl.DeviceIdType.MESH,
    )


def signal(sem, head, tile):
    pl.semaphore_signal(
        sem, inc=1, device_id={"head": head, "tile": tile},
        device_id_type=pl.DeviceIdType.MESH,
    )


def spread_kernel(
    nh, nt, chunks, a_ref, g_ref, mirror, own, parts, corr,
    msend, mrecv, psend, precv, gsend, grecv, lsem,
):
    maps, width, cols = a_ref.shape
    band = g_ref.shape[2]
    per = maps // chunks
    bands = cols // band
    nd = nh * nt
    h = lax.axis_index("head")
    t = lax.axis_index("tile")
    me = h * nt + t
    barrier = pltpu.get_barrier_semaphore()

    def greet(k, _):
        d = lax.rem(me + k, nd)
        signal(barrier, d // nt, lax.rem(d, nt))
        return 0

    lax.fori_loop(1, nd, greet, 0)

    ones_t = jnp.ones((8, cols), jnp.bfloat16)
    ones_w = jnp.ones((8, width), jnp.bfloat16)

    def partial_sums(c, _):
        a = a_ref[c]
        rows = lax.dot_general(
            ones_t, a, (((1,), (1,)), ((), ())), preferred_element_type=jnp.float32
        )
        own[c] = rows
        columns = jnp.dot(ones_w, a, preferred_element_type=jnp.float32)
        at = pl.ds(pl.multiple_of(t * cols, cols), cols)
        own[c, :, at] = own[c, :, at] + columns
        return 0

    def mirror_copy(k, q):
        p = lax.rem(t + k, nt)
        return remote(
            a_ref.at[pl.ds(q * per, per), pl.ds(pl.multiple_of(p * cols, cols), cols), :],
            mirror.at[t, pl.ds(q * per, per)],
            msend.at[q, k - 1], mrecv.at[q, k - 1], h, p,
        )

    def parts_copy(k):
        p = lax.rem(t + k, nt)
        return remote(own, parts.at[k - 1], psend.at[k - 1], precv.at[k - 1], h, p)

    pl.semaphore_wait(barrier, nd - 1)
    for q in range(chunks):
        for k in range(1, nt):
            mirror_copy(k, q).start()
    lax.fori_loop(0, maps, partial_sums, 0)
    for k in range(1, nt):
        parts_copy(k).start()
    for k in range(1, nt):
        parts_copy(k).wait()

    for q in range(chunks):
        for k in range(1, nt):
            mirror_copy(k, q).wait()

        def one_map(c, _):
            sums = own[c]
            for k in range(1, nt):
                sums = sums + parts[k - 1, c]
            own[c] = sums
            total = jnp.sum(sums[0:1], axis=1, keepdims=True)
            at = pl.ds(pl.multiple_of(t * cols, cols), cols)
            scaled = own[c, 0:1, at] / total
            for p in range(nt):
                rows = pl.ds(p * cols, cols)
                block = jnp.where(p == t, a_ref[c, rows, :], mirror[p, c])
                sym = a_ref[c, rows, :].astype(jnp.float32) + block.astype(jnp.float32).T
                r = jnp.broadcast_to(own[c, 0:1, rows], (cols, cols)).T
                value = (sym - r * scaled).astype(jnp.bfloat16)
                corr[q, pl.ds(p * bands, bands), c - q * per] = value.reshape(bands, band, cols)
            return 0

        lax.fori_loop(q * per, (q + 1) * per, one_map, 0)

        def ship(k, _):
            d = lax.rem(me + k, nd)
            remote(
                corr.at[q, d], g_ref.at[me, pl.ds(q * per, per)],
                gsend, grecv, d // nt, lax.rem(d, nt),
            ).start()
            return 0

        lax.fori_loop(1, nd, ship, 0)
        pltpu.make_async_copy(corr.at[q, me], g_ref.at[me, pl.ds(q * per, per)], lsem.at[q]).start()

    for q in range(chunks):
        pltpu.make_async_copy(corr.at[q, me], g_ref.at[me, pl.ds(q * per, per)], lsem.at[q]).wait()
    rest = g_ref.at[pl.ds(0, nd - 1)]
    pltpu.make_async_copy(rest, rest, gsend).wait()
    pltpu.make_async_copy(rest, rest, grecv).wait()


def spread(attention):
    nh, nt = lax.axis_size("head"), lax.axis_size("tile")
    nd = nh * nt
    maps, width, cols = attention.shape
    chunks = 3 if maps % 3 == 0 else 1
    band = width // nd
    far = max(nt - 1, 1)
    return pl.pallas_call(
        functools.partial(spread_kernel, nh, nt, chunks),
        out_shape=jax.ShapeDtypeStruct((nd, maps, band, cols), jnp.bfloat16),
        in_specs=[pl.BlockSpec(memory_space=VM)],
        out_specs=pl.BlockSpec(memory_space=VM),
        scratch_shapes=[
            VM((nt, maps, cols, cols), jnp.bfloat16),
            VM((maps, 8, width), jnp.float32),
            VM((far, maps, 8, width), jnp.float32),
            VM((chunks, nd, maps // chunks, band, cols), jnp.bfloat16),
            pltpu.SemaphoreType.DMA((chunks, far)),
            pltpu.SemaphoreType.DMA((chunks, far)),
            pltpu.SemaphoreType.DMA((far,)),
            pltpu.SemaphoreType.DMA((far,)),
            pltpu.SemaphoreType.DMA,
            pltpu.SemaphoreType.DMA,
            pltpu.SemaphoreType.DMA((chunks,)),
        ],
        compiler_params=pltpu.CompilerParams(
            collective_id=0, has_side_effects=True, vmem_limit_bytes=48 * 1024 * 1024
        ),
        name="spread",
    )(attention)


def stack_kernel(
    nh, nt, x_ref, pw_ref, pb_ref, cw_ref, cb_ref, ow_ref, out_ref,
    stream, hidden, taps, logits, hsend, hrecv, lsend, lrecv, csem,
):
    band, maps, width = x_ref.shape
    feat = pw_ref.shape[0]
    layers = cw_ref.shape[0]
    halo = 2 * layers
    rows = band + 2 * halo
    nd = nh * nt
    h = lax.axis_index("head")
    t = lax.axis_index("tile")
    me = h * nt + t
    up = lax.rem(me + nd - 1, nd)
    down = lax.rem(me + 1, nd)
    barrier = pltpu.get_barrier_semaphore()
    signal(barrier, up // nt, lax.rem(up, nt))
    signal(barrier, down // nt, lax.rem(down, nt))
    for k in range(1, nt):
        signal(barrier, h, lax.rem(t + k, nt))

    def project(r, _):
        value = jnp.dot(pw_ref[...], x_ref[r], preferred_element_type=jnp.float32)
        stream[halo + r] = (value + pb_ref[...]).astype(jnp.bfloat16)
        return 0

    lax.fori_loop(0, band, project, 0)
    pl.semaphore_wait(barrier, nt + 1)

    to_up = remote(
        stream.at[pl.ds(halo, halo)], stream.at[pl.ds(halo + band, halo)],
        hsend.at[0], hrecv.at[0], up // nt, lax.rem(up, nt),
    )
    to_down = remote(
        stream.at[pl.ds(band, halo)], stream.at[pl.ds(0, halo)],
        hsend.at[1], hrecv.at[1], down // nt, lax.rem(down, nt),
    )
    to_up.start()
    to_down.start()
    to_up.wait()
    to_down.wait()

    lane = lax.broadcasted_iota(jnp.int32, (feat, width), 1)
    first = me * band - halo

    def tap(source, dim, r, inside):
        v = source[r].astype(jnp.float32)
        if inside:
            g = first + r
            keep = jnp.logical_and(g >= 0, g < nd * band)
            v = jnp.where(keep, v, 0.0)
        before = jnp.where(lane == 0, 0.0, pltpu.roll(v, 1, 1))
        after = jnp.where(lane == width - 1, 0.0, pltpu.roll(v, width - 1, 1))
        stacked = jnp.concatenate(
            [before.astype(jnp.bfloat16), v.astype(jnp.bfloat16), after.astype(jnp.bfloat16)], axis=0
        )
        taps[r] = jnp.dot(cw_ref[dim[0], dim[1]], stacked, preferred_element_type=jnp.float32)

    for layer in range(layers):
        for half in range(2):
            low = 2 * layer + half
            source = hidden if half else stream

            def taps_of(r, _, source=source, layer=layer, half=half):
                tap(source, (layer, half), r, True)
                return 0

            lax.fori_loop(low, rows - low, taps_of, 0)

            def gather(r, _, layer=layer, half=half):
                conv = (
                    taps[r - 1, 0:feat] + taps[r, feat : 2 * feat] + taps[r + 1, 2 * feat :]
                    + cb_ref[layer, half]
                )
                if half:
                    stream[r] = (stream[r].astype(jnp.float32) + conv).astype(jnp.bfloat16)
                else:
                    hidden[r] = jnp.where(
                        conv > 0.0, conv, jnp.exp(jnp.minimum(conv, 0.0)) - 1.0
                    ).astype(jnp.bfloat16)
                return 0

            lax.fori_loop(low + 1, rows - low - 1, gather, 0)

    cols = width // nt
    for r in range(band):
        line = jnp.sum(stream[halo + r].astype(jnp.float32) * ow_ref[...], axis=0, keepdims=True)
        for p in range(nt):
            logits[p, r : r + 1, :] = line[:, p * cols : (p + 1) * cols]

    def deliver(k):
        p = lax.rem(t + k, nt)
        return remote(
            logits.at[p], out_ref.at[t], lsend.at[k - 1], lrecv.at[k - 1], h, p,
        )

    for k in range(1, nt):
        deliver(k).start()
    keep = pltpu.make_async_copy(logits.at[t], out_ref.at[t], csem)
    keep.start()
    keep.wait()
    for k in range(1, nt):
        deliver(k).wait()


def stack(x, pw, pb, cw, cb, ow):
    nh, nt = lax.axis_size("head"), lax.axis_size("tile")
    band, maps, width = x.shape
    feat = pw.shape[0]
    rows = band + 4 * cw.shape[0]
    far = max(nt - 1, 1)
    return pl.pallas_call(
        functools.partial(stack_kernel, nh, nt),
        out_shape=jax.ShapeDtypeStruct((nt, band, width // nt), jnp.float32),
        in_specs=[pl.BlockSpec(memory_space=VM)] * 6,
        out_specs=pl.BlockSpec(memory_space=VM),
        scratch_shapes=[
            VM((rows, feat, width), jnp.bfloat16),
            VM((rows, feat, width), jnp.bfloat16),
            VM((rows, 3 * feat, width), jnp.float32),
            VM((nt, band, width // nt), jnp.float32),
            pltpu.SemaphoreType.DMA((2,)),
            pltpu.SemaphoreType.DMA((2,)),
            pltpu.SemaphoreType.DMA((far,)),
            pltpu.SemaphoreType.DMA((far,)),
            pltpu.SemaphoreType.DMA,
        ],
        compiler_params=pltpu.CompilerParams(
            collective_id=1, has_side_effects=True, vmem_limit_bytes=48 * 1024 * 1024
        ),
        name="stack",
    )(x, pw, pb, cw, cb, ow)


def on_device(attention, proj_weight, proj_bias, conv_weight, conv_bias, out_weight):
    nh, nt = lax.axis_size("head"), lax.axis_size("tile")
    maps, width, cols = attention.shape
    grouped = spread(attention)
    band = grouped.shape[2]
    grouped = grouped.reshape(nh, nt, maps, band, cols)
    x = jnp.transpose(grouped, (3, 0, 2, 1, 4)).reshape(band, nh * maps, width)
    layers, two, feat = conv_weight.shape[:3]
    cw = jnp.transpose(conv_weight, (0, 1, 4, 2, 5, 3)).reshape(layers, two, 3 * feat, 3 * feat)
    out = stack(
        x, proj_weight, proj_bias[:, None], cw, conv_bias[..., None], out_weight[:, None]
    )
    return out.reshape(nt * band, cols)


def solution(mesh):
    return jax.shard_map(
        on_device,
        mesh=mesh,
        in_specs=(P(("grp", "head"), None, "tile"), P(), P(), P(), P(), P()),
        out_specs=P(("grp", "head"), "tile"),
        check_vma=False,
    )
```

```python
import functools
import jax
import jax.numpy as jnp
from jax import lax
from jax.experimental import pallas as pl
from jax.experimental.pallas import tpu as pltpu
from jax.sharding import PartitionSpec as P

VM = pltpu.VMEM
GROUP = 4


def remote(src, dst, send, recv, head, tile):
    return pltpu.make_async_remote_copy(
        src_ref=src,
        dst_ref=dst,
        send_sem=send,
        recv_sem=recv,
        device_id={"head": head, "tile": tile},
        device_id_type=pl.DeviceIdType.MESH,
    )


def sweep(low, high, body):
    groups = (high - low) // GROUP

    def step(i, _):
        body(low + i * GROUP, GROUP)
        return 0

    if groups:
        lax.fori_loop(0, groups, step, 0)
    if low + groups * GROUP < high:
        body(low + groups * GROUP, high - low - groups * GROUP)


def kernel(
    nh, nt, chunks, a_hbm, pw_ref, pb_ref, cw_hbm, cb_ref, ow_ref, out_ref,
    a_ref, cw_ref, mirror, own, parts, corr, got, wide, weights, stream, hidden, taps, logits,
    asem, wsem, msend, mrecv, psend, precv, gsend, grecv, lsem,
    hsend, hrecv, osend, orecv, csem,
):
    maps, width, cols = a_ref.shape
    band = got.shape[2]
    per = maps // chunks
    bands = cols // band
    nd = nh * nt
    feat = pw_ref.shape[0]
    layers = cw_ref.shape[0]
    halo = 2 * layers
    rows = band + 2 * halo
    h = lax.axis_index("head")
    t = lax.axis_index("tile")
    me = h * nt + t
    up = lax.rem(me + nd - 1, nd)
    down = lax.rem(me + 1, nd)

    load = pltpu.make_async_copy(a_hbm, a_ref, asem)
    load.start()
    load_weights = pltpu.make_async_copy(cw_hbm, cw_ref, wsem)
    load_weights.start()
    barrier = pltpu.get_barrier_semaphore()

    def greet(k, _):
        d = lax.rem(me + k, nd)
        pl.semaphore_signal(
            barrier, inc=1, device_id={"head": d // nt, "tile": lax.rem(d, nt)},
            device_id_type=pl.DeviceIdType.MESH,
        )
        return 0

    lax.fori_loop(1, nd, greet, 0)
    load.wait()
    mine = pl.ds(pl.multiple_of(t * cols, cols), cols)
    ones_t = jnp.ones((8, cols), jnp.bfloat16)
    ones_w = jnp.ones((8, width), jnp.bfloat16)

    def mirror_copy(k, q):
        p = lax.rem(t + k, nt)
        return remote(
            a_ref.at[pl.ds(q * per, per), pl.ds(pl.multiple_of(p * cols, cols), cols), :],
            mirror.at[t, pl.ds(q * per, per)],
            msend.at[q, k - 1], mrecv.at[q, k - 1], h, p,
        )

    def parts_copy(k):
        p = lax.rem(t + k, nt)
        return remote(own, parts.at[k - 1], psend.at[k - 1], precv.at[k - 1], h, p)

    def partial_sums(i, _):
        for j in range(per):
            c = i * per + j
            a = a_ref[c]
            line = lax.dot_general(
                ones_t, a, (((1,), (1,)), ((), ())), preferred_element_type=jnp.float32
            )
            own[c] = line
            columns = jnp.dot(ones_w, a, preferred_element_type=jnp.float32)
            own[c, :, mine] = own[c, :, mine] + columns
            mirror[t, c] = a_ref[c, mine, :]
        return 0

    pl.semaphore_wait(barrier, nd - 1)
    for q in range(chunks):
        for k in range(1, nt):
            mirror_copy(k, q).start()
    lax.fori_loop(0, chunks, partial_sums, 0)
    for k in range(1, nt):
        parts_copy(k).start()

    load_weights.wait()
    for layer in range(layers):
        for half in range(2):
            for dy in range(3):
                weights[layer, half, dy * feat : (dy + 1) * feat, :] = jnp.concatenate(
                    [cw_ref[layer, half, dy, dx].astype(jnp.float32) for dx in range(3)], axis=1
                ).astype(jnp.bfloat16)

    for k in range(1, nt):
        parts_copy(k).wait()

    for q in range(chunks):
        for k in range(1, nt):
            mirror_copy(k, q).wait()

        def one_map(c, slot, q=q):
            sums = own[c]
            for k in range(1, nt):
                sums = sums + parts[k - 1, c]
            own[c] = sums
            total = jnp.sum(sums, axis=1, keepdims=True)
            scaled = (own[c, :, mine] / total).T[:, 0:1]
            for p in range(nt):
                at = pl.ds(p * cols, cols)
                turned = mirror[p, c].astype(jnp.float32) - scaled * own[c, 0:1, at]
                value = (a_ref[c, at, :].astype(jnp.float32) + turned.T).astype(jnp.bfloat16)
                corr[q, pl.ds(p * bands, bands), slot] = value.reshape(bands, band, cols)

        for j in range(per):
            one_map(q * per + j, j)

        def ship(k, _, q=q):
            d = lax.rem(me + k, nd)
            remote(
                corr.at[q, d], got.at[me, pl.ds(q * per, per)],
                gsend, grecv, d // nt, lax.rem(d, nt),
            ).start()
            return 0

        lax.fori_loop(1, nd, ship, 0)
        pltpu.make_async_copy(corr.at[q, me], got.at[me, pl.ds(q * per, per)], lsem.at[q]).start()

    for q in range(chunks):
        pltpu.make_async_copy(corr.at[q, me], got.at[me, pl.ds(q * per, per)], lsem.at[q]).wait()
    rest = got.at[pl.ds(0, nd - 1)]
    pltpu.make_async_copy(rest, rest, grecv).wait()

    def unpack(i, _):
        for p in range(nt):
            wide[p, pl.ds(i * maps * band, maps * band), :] = (
                got[i * nt + p].astype(jnp.float32).reshape(maps * band, cols)
            )
        return 0

    lax.fori_loop(0, nh, unpack, 0)
    for r in range(band):
        x = jnp.concatenate(
            [wide[p, pl.ds(r, nh * maps, stride=band), :] for p in range(nt)], axis=1
        ).astype(jnp.bfloat16)
        value = jnp.dot(pw_ref[...], x, preferred_element_type=jnp.float32)
        stream[halo + r] = (value + pb_ref[...]).astype(jnp.bfloat16)

    to_up = remote(
        stream.at[pl.ds(halo, halo)], stream.at[pl.ds(halo + band, halo)],
        hsend.at[0], hrecv.at[0], up // nt, lax.rem(up, nt),
    )
    to_down = remote(
        stream.at[pl.ds(band, halo)], stream.at[pl.ds(0, halo)],
        hsend.at[1], hrecv.at[1], down // nt, lax.rem(down, nt),
    )
    to_up.start()
    to_down.start()

    lane = lax.broadcasted_iota(jnp.int32, (feat, width), 1)
    first = me * band - halo

    def taps_of(source, layer, half):
        def body(r, count):
            pieces = []
            for j in range(count):
                g = first + r + j
                keep = jnp.logical_and(g >= 0, g < nd * band)
                v = jnp.where(keep, source[r + j].astype(jnp.float32), 0.0)
                before = jnp.where(lane == 0, 0.0, pltpu.roll(v, 1, 1))
                after = jnp.where(lane == width - 1, 0.0, pltpu.roll(v, width - 1, 1))
                pieces.append(
                    jnp.concatenate(
                        [before.astype(jnp.bfloat16), v.astype(jnp.bfloat16), after.astype(jnp.bfloat16)],
                        axis=0,
                    )
                )
            block = jnp.dot(
                weights[layer, half], jnp.concatenate(pieces, axis=1),
                preferred_element_type=jnp.float32,
            )
            for j in range(count):
                taps[r + j] = block[:, j * width : (j + 1) * width]

        return body

    def gather_of(layer, half):
        bias = cb_ref[layer, half]

        def body(r, count):
            for j in range(count):
                s = r + j
                conv = (
                    taps[s - 1, 0:feat] + taps[s, feat : 2 * feat] + taps[s + 1, 2 * feat :] + bias
                )
                if half:
                    stream[s] = (stream[s].astype(jnp.float32) + conv).astype(jnp.bfloat16)
                else:
                    hidden[s] = jnp.where(
                        conv > 0.0, conv, jnp.exp(jnp.minimum(conv, 0.0)) - 1.0
                    ).astype(jnp.bfloat16)

        return body

    for layer in range(layers):
        for half in range(2):
            low = 2 * layer + half
            body = taps_of(hidden if half else stream, layer, half)
            if low:
                sweep(low, rows - low, body)
            else:
                sweep(halo, halo + band, body)
                to_up.wait()
                to_down.wait()
                sweep(0, halo, body)
                sweep(halo + band, rows, body)
            sweep(low + 1, rows - low - 1, gather_of(layer, half))

    for r in range(band):
        line = jnp.sum(stream[halo + r].astype(jnp.float32) * ow_ref[...], axis=0, keepdims=True)
        for p in range(nt):
            logits[p, r : r + 1, :] = line[:, p * cols : (p + 1) * cols]

    def deliver(k):
        p = lax.rem(t + k, nt)
        return remote(
            logits.at[p], out_ref.at[t], osend.at[k - 1], orecv.at[k - 1], h, p,
        )

    for k in range(1, nt):
        deliver(k).start()
    keep_own = pltpu.make_async_copy(logits.at[t], out_ref.at[t], csem)
    keep_own.start()
    keep_own.wait()
    for k in range(1, nt):
        deliver(k).wait()
    pltpu.make_async_copy(rest, rest, gsend).wait()


def on_device(attention, proj_weight, proj_bias, conv_weight, conv_bias, out_weight):
    nh, nt = lax.axis_size("head"), lax.axis_size("tile")
    nd = nh * nt
    maps, width, cols = attention.shape
    layers, two, feat = conv_weight.shape[:3]
    chunks = 3 if maps % 3 == 0 else 1
    band = width // nd
    far = max(nt - 1, 1)
    rows = band + 4 * layers
    ordered = jnp.transpose(conv_weight, (0, 1, 4, 5, 2, 3))
    dma = pltpu.SemaphoreType.DMA
    out = pl.pallas_call(
        functools.partial(kernel, nh, nt, chunks),
        out_shape=jax.ShapeDtypeStruct((nt, band, cols), jnp.float32),
        in_specs=[
            pl.BlockSpec(memory_space=pltpu.HBM),
            pl.BlockSpec(memory_space=VM),
            pl.BlockSpec(memory_space=VM),
            pl.BlockSpec(memory_space=pltpu.HBM),
            pl.BlockSpec(memory_space=VM),
            pl.BlockSpec(memory_space=VM),
        ],
        out_specs=pl.BlockSpec(memory_space=VM),
        scratch_shapes=[
            VM((maps, width, cols), jnp.bfloat16),
            VM(ordered.shape, jnp.bfloat16),
            VM((nt, maps, cols, cols), jnp.bfloat16),
            VM((maps, 8, width), jnp.float32),
            VM((far, maps, 8, width), jnp.float32),
            VM((chunks, nd, maps // chunks, band, cols), jnp.bfloat16),
            VM((nd, maps, band, cols), jnp.bfloat16),
            VM((nt, nh * maps * band, cols), jnp.float32),
            VM((layers, two, 3 * feat, 3 * feat), jnp.bfloat16),
            VM((rows, feat, width), jnp.bfloat16),
            VM((rows, feat, width), jnp.bfloat16),
            VM((rows, 3 * feat, width), jnp.float32),
            VM((nt, band, cols), jnp.float32),
            dma,
            dma,
            dma((chunks, far)),
            dma((chunks, far)),
            dma((far,)),
            dma((far,)),
            dma,
            dma,
            dma((chunks,)),
            dma((2,)),
            dma((2,)),
            dma((far,)),
            dma((far,)),
            dma,
        ],
        compiler_params=pltpu.CompilerParams(
            collective_id=0, has_side_effects=True, vmem_limit_bytes=56 * 1024 * 1024
        ),
        name="head",
    )(
        attention, proj_weight, proj_bias[:, None], ordered, conv_bias[..., None],
        out_weight[:, None],
    )
    return out.reshape(nt * band, cols)


def solution(mesh):
    return jax.shard_map(
        on_device,
        mesh=mesh,
        in_specs=(P(("grp", "head"), None, "tile"), P(), P(), P(), P(), P()),
        out_specs=P(("grp", "head"), "tile"),
        check_vma=False,
    )
```

```python
import functools
import jax
import jax.numpy as jnp
from jax import lax
from jax.experimental import pallas as pl
from jax.experimental.pallas import tpu as pltpu
from jax.sharding import PartitionSpec as P

VM = pltpu.VMEM
GROUP = 4


def remote(src, dst, send, recv, head, tile):
    return pltpu.make_async_remote_copy(
        src_ref=src,
        dst_ref=dst,
        send_sem=send,
        recv_sem=recv,
        device_id={"head": head, "tile": tile},
        device_id_type=pl.DeviceIdType.MESH,
    )


def band_of(head, tile, nt):
    block, core = head // 2, lax.rem(head, 2)
    u = jnp.where(lax.rem(block, 2) == 0, tile, nt - 1 - tile)
    core = jnp.where(lax.rem(u, 2) == 0, core, 1 - core)
    return block * (2 * nt) + 2 * u + core


def place_of(band, nt):
    block, spot = band // (2 * nt), lax.rem(band, 2 * nt)
    u, core = spot // 2, lax.rem(spot, 2)
    core = jnp.where(lax.rem(u, 2) == 0, core, 1 - core)
    return block * 2 + core, jnp.where(lax.rem(block, 2) == 0, u, nt - 1 - u)


def sweep(low, high, body):
    groups = (high - low) // GROUP

    def step(i, _):
        body(low + i * GROUP, GROUP)
        return 0

    if groups:
        lax.fori_loop(0, groups, step, 0)
    if low + groups * GROUP < high:
        body(low + groups * GROUP, high - low - groups * GROUP)


def kernel(
    nh, nt, chunks, a_hbm, pw_ref, pb_ref, cw_hbm, cb_ref, ow_ref, out_ref,
    a_ref, cw_ref, mirror, own, total_of, parts, corr, got, wide, weights, stream, hidden, taps, logits,
    asem, wsem, msend, mrecv, psend, precv, gsend, grecv, lsem,
    hsend, hrecv, osend, orecv,
):
    maps, width, cols = a_ref.shape
    band = got.shape[2]
    per = maps // chunks
    bands = cols // band
    nd = nh * nt
    feat = pw_ref.shape[0]
    layers = cw_ref.shape[0]
    halo = 2 * layers
    rows = band + 2 * halo
    h = lax.axis_index("head")
    t = lax.axis_index("tile")
    me = h * nt + t
    spot = band_of(h, t, nt)
    up_head, up_tile = place_of(lax.rem(spot + nd - 1, nd), nt)
    down_head, down_tile = place_of(lax.rem(spot + 1, nd), nt)

    load = pltpu.make_async_copy(a_hbm, a_ref, asem)
    load.start()
    load_weights = pltpu.make_async_copy(cw_hbm, cw_ref, wsem)
    load_weights.start()
    barrier = pltpu.get_barrier_semaphore()

    def others(visit):
        def step(i, _):
            head = lax.rem(h + i, nh)
            for k in range(nt):
                visit(head, lax.rem(t + k, nt))
            return 0

        for k in range(1, nt):
            visit(h, lax.rem(t + k, nt))
        lax.fori_loop(1, nh, step, 0)

    def greet(head, tile):
        pl.semaphore_signal(
            barrier, inc=1, device_id={"head": head, "tile": tile},
            device_id_type=pl.DeviceIdType.MESH,
        )

    others(greet)
    load.wait()
    mine = pl.ds(pl.multiple_of(t * cols, cols), cols)
    ones_t = jnp.ones((8, cols), jnp.bfloat16)
    ones_w = jnp.ones((8, width), jnp.bfloat16)

    def mirror_copy(k, q):
        p = lax.rem(t + k, nt)
        return remote(
            a_ref.at[pl.ds(q * per, per), pl.ds(pl.multiple_of(p * cols, cols), cols), :],
            mirror.at[t, pl.ds(q * per, per)],
            msend.at[q, k - 1], mrecv.at[q, k - 1], h, p,
        )

    def parts_copy(k):
        p = lax.rem(t + k, nt)
        return remote(own, parts.at[k - 1], psend.at[k - 1], precv.at[k - 1], h, p)

    def partial_sums(i, _):
        for j in range(per):
            c = i * per + j
            a = a_ref[c]
            line = lax.dot_general(
                ones_t, a, (((1,), (1,)), ((), ())), preferred_element_type=jnp.float32
            )
            own[c] = line[0:1]
            columns = jnp.dot(ones_w, a, preferred_element_type=jnp.float32)
            own[c, :, mine] = own[c, :, mine] + columns[0:1]
            mirror[t, c] = a_ref[c, mine, :]
        return 0

    lax.fori_loop(0, chunks, partial_sums, 0)

    def upright(line):
        return jnp.broadcast_to(line, (8, feat)).T[:, 0:1]

    load_weights.wait()
    for layer in range(layers):
        for half in range(2):
            for dy in range(3):
                weights[layer, half, dy * feat : (dy + 1) * feat, :] = jnp.concatenate(
                    [cw_ref[layer, half, dy, dx].astype(jnp.float32) for dx in range(3)], axis=1
                ).astype(jnp.bfloat16)

    pl.semaphore_wait(barrier, nd - 1)
    for k in range(1, nt):
        parts_copy(k).start()
    for q in range(chunks):
        for k in range(1, nt):
            mirror_copy(k, q).start()
    for k in range(1, nt):
        parts_copy(k).wait()

    for q in range(chunks):
        for k in range(1, nt):
            mirror_copy(k, q).wait()

        def one_map(c, slot, q=q):
            sums = own[c]
            for k in range(1, nt):
                sums = sums + parts[k - 1, c]
            total_of[c] = sums
            total = jnp.sum(sums, axis=1, keepdims=True)
            scaled = jnp.broadcast_to(total_of[c, :, mine] / total, (8, cols)).T[:, 0:1]
            for p in range(nt):
                at = pl.ds(p * cols, cols)
                turned = mirror[p, c].astype(jnp.float32) - scaled * total_of[c, :, at]
                value = (a_ref[c, at, :].astype(jnp.float32) + turned.T).astype(jnp.bfloat16)
                corr[q, pl.ds(p * bands, bands), slot] = value.reshape(bands, band, cols)

        for j in range(per):
            one_map(q * per + j, j)

        def ship(head, tile, q=q):
            remote(
                corr.at[q, band_of(head, tile, nt)], got.at[me, pl.ds(q * per, per)],
                gsend, grecv, head, tile,
            ).start()

        others(ship)
        pltpu.make_async_copy(corr.at[q, spot], got.at[me, pl.ds(q * per, per)], lsem.at[q]).start()

    for q in range(chunks):
        pltpu.make_async_copy(corr.at[q, spot], got.at[me, pl.ds(q * per, per)], lsem.at[q]).wait()
    rest = got.at[pl.ds(0, nd - 1)]
    pltpu.make_async_copy(rest, rest, grecv).wait()

    def unpack(i, _):
        for p in range(nt):
            wide[p, pl.ds(i * maps * band, maps * band), :] = (
                got[i * nt + p].astype(jnp.float32).reshape(maps * band, cols)
            )
        return 0

    lax.fori_loop(0, nh, unpack, 0)
    proj_bias = upright(pb_ref[...])
    for r in range(band):
        x = jnp.concatenate(
            [wide[p, pl.ds(r, nh * maps, stride=band), :] for p in range(nt)], axis=1
        ).astype(jnp.bfloat16)
        value = jnp.dot(pw_ref[...], x, preferred_element_type=jnp.float32)
        stream[halo + r] = (value + proj_bias).astype(jnp.bfloat16)

    to_up = remote(
        stream.at[pl.ds(halo, halo)], stream.at[pl.ds(halo + band, halo)],
        hsend.at[0], hrecv.at[0], up_head, up_tile,
    )
    to_down = remote(
        stream.at[pl.ds(band, halo)], stream.at[pl.ds(0, halo)],
        hsend.at[1], hrecv.at[1], down_head, down_tile,
    )
    to_up.start()
    to_down.start()

    lane = lax.broadcasted_iota(jnp.int32, (feat, width), 1)
    first = spot * band - halo

    def taps_of(source, layer, half):
        def body(r, count):
            pieces = []
            for j in range(count):
                g = first + r + j
                keep = jnp.logical_and(g >= 0, g < nd * band)
                v = jnp.where(keep, source[r + j].astype(jnp.float32), 0.0)
                before = jnp.where(lane == 0, 0.0, pltpu.roll(v, 1, 1))
                after = jnp.where(lane == width - 1, 0.0, pltpu.roll(v, width - 1, 1))
                pieces.append(
                    jnp.concatenate(
                        [before.astype(jnp.bfloat16), v.astype(jnp.bfloat16), after.astype(jnp.bfloat16)],
                        axis=0,
                    )
                )
            block = jnp.dot(
                weights[layer, half], jnp.concatenate(pieces, axis=1),
                preferred_element_type=jnp.float32,
            )
            for j in range(count):
                taps[r + j] = block[:, j * width : (j + 1) * width]

        return body

    def gather_of(layer, half):
        bias = upright(cb_ref[layer, half : half + 1, :])

        def body(r, count):
            for j in range(count):
                s = r + j
                conv = (
                    taps[s - 1, 0:feat] + taps[s, feat : 2 * feat] + taps[s + 1, 2 * feat :] + bias
                )
                if half:
                    stream[s] = (stream[s].astype(jnp.float32) + conv).astype(jnp.bfloat16)
                else:
                    hidden[s] = jnp.where(
                        conv > 0.0, conv, jnp.exp(jnp.minimum(conv, 0.0)) - 1.0
                    ).astype(jnp.bfloat16)

        return body

    for layer in range(layers):
        for half in range(2):
            low = 2 * layer + half
            body = taps_of(hidden if half else stream, layer, half)
            if low:
                sweep(low, rows - low, body)
            else:
                sweep(halo, halo + band, body)
                to_up.wait()
                to_down.wait()
                sweep(0, halo, body)
                sweep(halo + band, rows, body)
            sweep(low + 1, rows - low - 1, gather_of(layer, half))

    readout = upright(ow_ref[...])
    for r in range(band):
        line = jnp.sum(stream[halo + r].astype(jnp.float32) * readout, axis=0, keepdims=True)
        for p in range(nt):
            logits[p, r : r + 1, :] = line[:, p * cols : (p + 1) * cols]

    owner, slot = spot // nt, lax.rem(spot, nt)

    def deliver(k):
        p = lax.rem(t + k, nt)
        return remote(
            logits.at[p], out_ref.at[slot], osend.at[k], orecv.at[slot], owner, p,
        )

    for k in range(1, nt):
        deliver(k).start()

    @pl.when(owner == h)
    def _():
        pltpu.make_async_copy(logits.at[t], out_ref.at[slot], orecv.at[slot]).start()

    @pl.when(owner != h)
    def _():
        deliver(0).start()
        deliver(0).wait_send()

    for k in range(1, nt):
        deliver(k).wait_send()
    for k in range(nt):
        pltpu.make_async_copy(logits.at[k], out_ref.at[k], orecv.at[k]).wait()
    pltpu.make_async_copy(rest, rest, gsend).wait()


def on_device(attention, proj_weight, proj_bias, conv_weight, conv_bias, out_weight):
    nh, nt = lax.axis_size("head"), lax.axis_size("tile")
    nd = nh * nt
    maps, width, cols = attention.shape
    layers, two, feat = conv_weight.shape[:3]
    chunks = maps
    band = width // nd
    far = max(nt - 1, 1)
    rows = band + 4 * layers
    ordered = jnp.transpose(conv_weight, (0, 1, 4, 5, 2, 3))
    dma = pltpu.SemaphoreType.DMA
    out = pl.pallas_call(
        functools.partial(kernel, nh, nt, chunks),
        out_shape=jax.ShapeDtypeStruct((nt, band, cols), jnp.float32),
        in_specs=[
            pl.BlockSpec(memory_space=pltpu.HBM),
            pl.BlockSpec(memory_space=VM),
            pl.BlockSpec(memory_space=VM),
            pl.BlockSpec(memory_space=pltpu.HBM),
            pl.BlockSpec(memory_space=VM),
            pl.BlockSpec(memory_space=VM),
        ],
        out_specs=pl.BlockSpec(memory_space=VM),
        scratch_shapes=[
            VM((maps, width, cols), jnp.bfloat16),
            VM(ordered.shape, jnp.bfloat16),
            VM((nt, maps, cols, cols), jnp.bfloat16),
            VM((maps, 1, width), jnp.float32),
            VM((maps, 1, width), jnp.float32),
            VM((far, maps, 1, width), jnp.float32),
            VM((chunks, nd, maps // chunks, band, cols), jnp.bfloat16),
            VM((nd, maps, band, cols), jnp.bfloat16),
            VM((nt, nh * maps * band, cols), jnp.float32),
            VM((layers, two, 3 * feat, 3 * feat), jnp.bfloat16),
            VM((rows, feat, width), jnp.bfloat16),
            VM((rows, feat, width), jnp.bfloat16),
            VM((rows, 3 * feat, width), jnp.float32),
            VM((nt, band, cols), jnp.float32),
            dma,
            dma,
            dma((chunks, far)),
            dma((chunks, far)),
            dma((far,)),
            dma((far,)),
            dma,
            dma,
            dma((chunks,)),
            dma((2,)),
            dma((2,)),
            dma((nt,)),
            dma((nt,)),
        ],
        compiler_params=pltpu.CompilerParams(
            collective_id=0, has_side_effects=True, vmem_limit_bytes=56 * 1024 * 1024
        ),
        name="head",
    )(
        attention, proj_weight, proj_bias[None], ordered, conv_bias, out_weight[None],
    )
    return out.reshape(nt * band, cols)


def solution(mesh):
    return jax.shard_map(
        on_device,
        mesh=mesh,
        in_specs=(P(("grp", "head"), None, "tile"), P(), P(), P(), P(), P()),
        out_specs=P(("grp", "head"), "tile"),
        check_vma=False,
    )
```
